512 devices in a mesh: rep: 64 (over x, y, core), tp: 8 (over z).
Axes of the slice: x: 4, y: 8, z: 8, core: 2. Of those that a mesh axis runs over, the one named last changes fastest.
Arguments:
- queries: bfloat16 [4096, 2, 8192], P('rep', None, 'tp'), may hold values from -170 to 170
- step_keys: bfloat16 [4096, 2, 1024], P('rep', None, 'tp'), may hold values from -9 to 9
- step_values: bfloat16 [4096, 2, 1024], P('rep', None, 'tp'), may hold values from -6 to 6
- suffix_keys: bfloat16 [4096, 64, 1024], P('rep', None, 'tp'), may hold values from -6 to 6
- suffix_values: bfloat16 [4096, 64, 1024], P('rep', None, 'tp'), may hold values from -6 to 6
- suffix_len: int32 [4096], P('rep'), may hold values from 1 to 64, as said below
- row_schema: int32 [4096], P('rep'), may hold values from 0 to 63, as said below
- held: int32 [64, 2], P('rep'), may hold values from 0 to 63, as said below
- dest_replica: int32 [4096], P('rep'), may hold values from 0 to 63, as said below
- dest_slot: int32 [4096], P('rep'), may hold values from 0 to 63, as said below
- prefix_keys: bfloat16 [64, 2, 2048, 1024], P('rep', None, 'tp'), may hold values from -6 to 6, as said below
- prefix_values: bfloat16 [64, 2, 2048, 1024], P('rep', None, 'tp'), may hold values from -6 to 6, as said below
Outputs:
- attended: bfloat16 [4096, 2, 8192], P('rep', None, 'tp')
The draws below stay inside these ranges and needn't reach their ends.
Inputs may be any that keep to these rules, and one draw needn't show every extreme that they name: Each schema stands in exactly 2 rows of held, never twice in one row. row_schema[r] is one of the schemas in held[dest_replica[r]]. `dest_replica`: every replica receives exactly 64 rows; of the rows of one replica at most 2 go to one replica, and every replica sends exactly 2 to some replica. The pairs (dest_replica, dest_slot) are all different. `suffix_len`: on every replica some row has exactly 64. `prefix_keys`: copies of one schema on different replicas are equal. `prefix_values`: copies of one schema on different replicas are equal.
All inputs are finite; a program needn't handle non-finite values.
Results may differ from the reference program's by a relative error of at most 0.0035.
Values may be sent and summed in bfloat16 or wider, within the bound.
A program may use at most 128 MiB of HBM per device.

```python
import jax
import jax.numpy as jnp
from jax import lax

H = 64
KVH = 8
HD = 128
PRE = 2048
SUF = 64
STEPS = 2
SLOTS = 2
ROWS_REP = 64
SCHEMAS = 64
CAP = 2
ROWS = 4096


def layout_tables(key):
    replicas = ROWS // ROWS_REP
    groups = replicas // 2
    sigma = jax.random.permutation(jax.random.fold_in(key, 1), replicas)
    offset = jax.random.randint(jax.random.fold_in(key, 2), (), 1, replicas)
    second = sigma[(jnp.arange(replicas) + offset) % replicas]
    held_table = jnp.stack([sigma, second], axis=1).astype(jnp.int32)
    common = jax.random.randint(jax.random.fold_in(key, 3), (), 0, replicas)
    perm_keys = jax.random.split(jax.random.fold_in(key, 4), CAP)
    rest = jax.vmap(lambda inner: jax.random.permutation(inner, replicas - 1))(perm_keys) + 1
    offsets = (common + jnp.concatenate([jnp.zeros((CAP, 1), jnp.int32), rest[:, :groups - 1].astype(jnp.int32)], axis=1)) % replicas
    row_keys = jax.random.split(jax.random.fold_in(key, 5), replicas)
    row_codes = jax.vmap(lambda inner: jax.random.permutation(inner, ROWS_REP))(row_keys).astype(jnp.int32)
    block_code = row_codes // groups
    group_code = row_codes % groups
    destination = (jnp.arange(replicas)[:, None] + offsets[block_code, group_code]) % replicas
    slot_keys = jax.random.split(jax.random.fold_in(key, 6), replicas)
    slot_perm = jax.vmap(lambda inner: jax.random.permutation(inner, ROWS_REP))(slot_keys).astype(jnp.int32)
    slots = slot_perm[destination, block_code * groups + group_code]
    which = jax.random.randint(jax.random.fold_in(key, 7), (replicas, ROWS_REP), 0, 2)
    schemas = held_table[destination, which]
    return (held_table, destination.reshape(-1).astype(jnp.int32), slots.reshape(-1).astype(jnp.int32), schemas.reshape(-1).astype(jnp.int32))


def draw_held(key, part):
    return layout_tables(key)[0]


def draw_dest_replica(key, part):
    return layout_tables(key)[1]


def draw_dest_slot(key, part):
    return layout_tables(key)[2]


def draw_row_schema(key, part):
    return layout_tables(key)[3]


def draw_suffix_len(key, part):
    replicas = ROWS // ROWS_REP
    lengths = jax.random.randint(jax.random.fold_in(key, 41), (replicas, ROWS_REP), 1, SUF + 1)
    longest = jax.random.randint(jax.random.fold_in(key, 42), (replicas, 1), 0, ROWS_REP)
    lengths = jnp.where(jnp.arange(ROWS_REP)[None, :] == longest, SUF, lengths)
    return lengths.reshape(-1).astype(jnp.int32)


def schema_cache(key, salt):
    held_table = layout_tables(key)[0]
    inner = jax.random.fold_in(key, salt)
    base = jnp.clip(jax.random.normal(inner, (SCHEMAS, PRE, KVH * HD), jnp.float32), -6.0, 6.0)
    return base.astype(jnp.bfloat16)[held_table]


def draw_prefix_keys(key, part):
    return schema_cache(key, 21)


def draw_prefix_values(key, part):
    return schema_cache(key, 22)


def draw_queries(key, part):
    inner = jax.random.fold_in(key, 31)
    base = jnp.clip(jax.random.normal(inner, (ROWS, STEPS, H * HD), jnp.float32), -6.0, 6.0) * 2.5
    return base.astype(jnp.bfloat16)


def shard_levels(own_key, shape, shards, smallest, top_value):
    gain = 1.0
    for axis_at, blocks in shards:
        steps = jax.random.uniform(jax.random.fold_in(jax.random.fold_in(own_key, 6), axis_at), (blocks,), jnp.float32, smallest / len(shards), top_value / len(shards))
        gain = gain * jnp.repeat(jnp.exp(steps), shape[axis_at] // blocks).reshape((-1,) + (1,) * (len(shape) - 1 - axis_at))
    return gain


def gaussian(key, shape, deviation, most, cuts=(), kind=jnp.bfloat16):
    level = shard_levels(key, shape, cuts, -0.22, 0.18) if cuts else 1.0
    drawn = jax.random.normal(key, shape, jnp.float32) * deviation * level
    return jnp.minimum(jnp.maximum(drawn, -most), most).astype(kind)


def setup_inputs(seed: int = 0) -> dict:
    keys = jax.random.split(jax.random.key(seed), 13)
    return {
        "queries": draw_queries(jax.random.fold_in(keys[12], 71), 0),
        "step_keys": gaussian(keys[1], (ROWS, STEPS, KVH * HD), 1.5, 9.0, ((0, 64), (2, 8))),
        "step_values": gaussian(keys[2], (ROWS, STEPS, KVH * HD), 1.0, 6.0, ((0, 64), (2, 8))),
        "suffix_keys": gaussian(keys[3], (ROWS, SUF, KVH * HD), 1.0, 6.0, ((0, 64), (2, 8))),
        "suffix_values": gaussian(keys[4], (ROWS, SUF, KVH * HD), 1.0, 6.0, ((0, 64), (2, 8))),
        "suffix_len": draw_suffix_len(jax.random.fold_in(keys[12], 71), 0),
        "row_schema": draw_row_schema(jax.random.fold_in(keys[12], 71), 0),
        "held": draw_held(jax.random.fold_in(keys[12], 71), 0),
        "dest_replica": draw_dest_replica(jax.random.fold_in(keys[12], 71), 0),
        "dest_slot": draw_dest_slot(jax.random.fold_in(keys[12], 71), 0),
        "prefix_keys": draw_prefix_keys(jax.random.fold_in(keys[12], 71), 0),
        "prefix_values": draw_prefix_values(jax.random.fold_in(keys[12], 71), 0),
    }


def reference(queries, step_keys, step_values, suffix_keys, suffix_values, suffix_len, row_schema, held, dest_replica, dest_slot, prefix_keys, prefix_values):
    block = 16
    group_size = H // KVH
    scale = HD ** -0.5
    chosen = held[dest_replica] == row_schema[:, None]
    slot_ids = jnp.sum(jnp.where(chosen, jnp.arange(SLOTS)[None, :], 0), axis=1).astype(jnp.int32)
    blocks = ROWS // block

    def shaped(values):
        return values.reshape((blocks, block) + values.shape[1:])

    def one_block(inputs):
        query_rows, own_keys, own_values, new_keys, new_values, lengths, replica_ids, slot_rows = inputs
        prefix_k = prefix_keys[replica_ids, slot_rows].astype(jnp.float32).reshape(block, PRE, KVH, HD)
        prefix_v = prefix_values[replica_ids, slot_rows].astype(jnp.float32).reshape(block, PRE, KVH, HD)
        query_heads = query_rows.astype(jnp.float32).reshape(block, STEPS, KVH, group_size, HD)
        prefix_scores = jnp.einsum("btkgd,bpkd->btkgp", query_heads, prefix_k) * scale
        key_rows = jnp.concatenate([own_keys, new_keys], axis=1).astype(jnp.float32).reshape(block, SUF + STEPS, KVH, HD)
        value_rows = jnp.concatenate([own_values, new_values], axis=1).astype(jnp.float32).reshape(block, SUF + STEPS, KVH, HD)
        own_scores = jnp.einsum("btkgd,bjkd->btkgj", query_heads, key_rows) * scale
        position = jnp.arange(SUF + STEPS)[None, None, :]
        step_index = jnp.arange(STEPS)[None, :, None]
        allowed = ((position < SUF) & (position < lengths[:, None, None])) | ((position >= SUF) & (position - SUF <= step_index))
        own_scores = jnp.where(allowed[:, :, None, None, :], own_scores, -jnp.inf)
        row_peak = jnp.maximum(jnp.max(prefix_scores, axis=-1), jnp.max(own_scores, axis=-1))
        prefix_weights = jnp.exp(prefix_scores - row_peak[..., None]).astype(jnp.bfloat16).astype(jnp.float32)
        own_weights = jnp.exp(own_scores - row_peak[..., None]).astype(jnp.bfloat16).astype(jnp.float32)
        totals = jnp.sum(prefix_weights, axis=-1) + jnp.sum(own_weights, axis=-1)
        weighted = jnp.einsum("btkgp,bpkd->btkgd", prefix_weights, prefix_v) + jnp.einsum("btkgj,bjkd->btkgd", own_weights, value_rows)
        return (weighted / totals[..., None]).astype(jnp.bfloat16).reshape(block, STEPS, H * HD)

    results = lax.map(one_block, (shaped(queries), shaped(suffix_keys), shaped(suffix_values), shaped(step_keys), shaped(step_values), shaped(suffix_len), shaped(dest_replica), shaped(slot_ids)))
    results = results.reshape(ROWS, STEPS, H * HD)
    target = (dest_replica * ROWS_REP + dest_slot).astype(jnp.int32)
    return jnp.zeros((ROWS, STEPS, H * HD), results.dtype).at[target].set(results)
```

```python
import jax
import jax.numpy as jnp
from jax import lax
from jax.sharding import PartitionSpec as P

HD = 128


def local_scores(query_rows, key_rows, lengths, suffix_count):
    row_count, step_count, width = query_rows.shape
    kv_count = key_rows.shape[2] // HD
    group_size = width // HD // kv_count
    query_heads = query_rows.reshape(row_count, step_count, kv_count, group_size, HD)
    key_heads = key_rows.reshape(row_count, key_rows.shape[1], kv_count, HD)
    scores = jnp.einsum(
        "rtkgd,rjkd->rtkgj", query_heads, key_heads, preferred_element_type=jnp.float32
    ) * HD ** (-0.5)
    position = jnp.arange(key_rows.shape[1])[None, None, :]
    step_index = jnp.arange(step_count)[None, :, None]
    allowed = (position < suffix_count) & (position < lengths[:, None, None]) | (
        position >= suffix_count
    ) & (position - suffix_count <= step_index)
    return jnp.where(allowed[:, :, None, None, :], scores, -jnp.inf)


def local_sums(scores, row_peak, value_rows):
    kv_count = scores.shape[2]
    weights = jnp.exp(scores - row_peak[..., None]).astype(jnp.bfloat16)
    value_heads = value_rows.reshape(value_rows.shape[0], value_rows.shape[1], kv_count, HD)
    weighted = jnp.einsum(
        "rtkgj,rjkd->rtkgd", weights, value_heads, preferred_element_type=jnp.float32
    )
    totals = jnp.sum(weights.astype(jnp.float32), axis=-1)
    return (weighted, totals)


def prefix_scores(query_rows, prefix_block, chosen):
    row_count, step_count, width = query_rows.shape
    slot_count, token_count = prefix_block.shape[0], prefix_block.shape[1]
    kv_count = prefix_block.shape[2] // HD
    group_size = width // HD // kv_count
    query_heads = query_rows.reshape(row_count, step_count, kv_count, group_size, HD)
    key_heads = prefix_block.reshape(slot_count * token_count, kv_count, HD)
    scores = jnp.einsum(
        "rtkgd,pkd->rtkgp", query_heads, key_heads, preferred_element_type=jnp.float32
    ) * HD ** (-0.5)
    allowed = jnp.repeat(chosen, token_count, axis=1)
    return jnp.where(allowed[:, None, None, None, :], scores, -jnp.inf)


def prefix_sums(scores, row_peak, value_block, chosen):
    kv_count = value_block.shape[2] // HD
    weights = jnp.exp(scores - row_peak[..., None]).astype(jnp.bfloat16)
    totals = jnp.sum(weights.astype(jnp.float32), axis=-1)
    value_heads = value_block.reshape(value_block.shape[0] * value_block.shape[1], kv_count, HD)
    weighted = jnp.einsum(
        "rtkgp,pkd->rtkgd", weights, value_heads, preferred_element_type=jnp.float32
    )
    return (weighted, totals)


def shards(
    queries,
    step_keys,
    step_values,
    suffix_keys,
    suffix_values,
    suffix_len,
    row_schema,
    held,
    dest_replica,
    dest_slot,
    prefix_keys,
    prefix_values,
):
    row_count = queries.shape[0]
    replicas = lax.axis_size("rep")
    capacity = 2 * row_count // replicas
    buffer_rows = replicas * capacity
    suffix_count = suffix_keys.shape[1]
    kv_local = step_keys.shape[2] // HD
    tp_index = lax.axis_index("tp")
    row_order = jnp.arange(row_count)
    earlier = (dest_replica[None, :] == dest_replica[:, None]) & (
        row_order[None, :] < row_order[:, None]
    )
    placed = dest_replica * capacity + jnp.sum(earlier.astype(jnp.int32), axis=1)

    def packed(values):
        return jnp.zeros((buffer_rows,) + values.shape[1:], values.dtype).at[placed].set(values)

    prefix_key_rows, prefix_value_rows = (prefix_keys[0], prefix_values[0])
    row_facts = jnp.stack([dest_slot + 1, row_schema, suffix_len], axis=1)
    row_facts = lax.all_to_all(packed(row_facts), "rep", split_axis=0, concat_axis=0, tiled=True)
    slot_plus, schemas, lengths = (row_facts[:, 0], row_facts[:, 1], row_facts[:, 2])
    target = jnp.arange(row_count) + 1
    matches = slot_plus[None, :] == target[:, None]
    arrived = jnp.sum(jnp.where(matches, jnp.arange(buffer_rows)[None, :], 0), axis=1)
    moved_queries, moved_step_keys, moved_step_values, moved_suffix_keys, moved_suffix_values = (
        lax.all_to_all(packed(queries), "rep", split_axis=0, concat_axis=0, tiled=True),
        lax.all_to_all(packed(step_keys), "rep", split_axis=0, concat_axis=0, tiled=True),
        lax.all_to_all(packed(step_values), "rep", split_axis=0, concat_axis=0, tiled=True),
        lax.all_to_all(packed(suffix_keys), "rep", split_axis=0, concat_axis=0, tiled=True),
        lax.all_to_all(packed(suffix_values), "rep", split_axis=0, concat_axis=0, tiled=True),
    )
    moved_queries = moved_queries[arrived]
    key_rows = jnp.concatenate([moved_suffix_keys[arrived], moved_step_keys[arrived]], axis=1)
    value_rows = jnp.concatenate([moved_suffix_values[arrived], moved_step_values[arrived]], axis=1)
    chosen = held[0][None, :] == schemas[arrived][:, None]
    suffix_scores = local_scores(moved_queries, key_rows, lengths[arrived], suffix_count)
    every_head = lax.all_gather(moved_queries, "tp", axis=2, tiled=True)
    scores = prefix_scores(every_head, prefix_key_rows, chosen)
    schema_max = jnp.max(scores, axis=-1)
    own_wide = jnp.full(schema_max.shape, -jnp.inf, jnp.float32)
    own_wide = lax.dynamic_update_slice_in_dim(
        own_wide, jnp.max(suffix_scores, axis=-1), tp_index * kv_local, 2
    )
    peak_all = lax.pmax(jnp.maximum(schema_max, own_wide), "tp")
    scores, row_peak, peak_all = (
        scores,
        lax.dynamic_slice_in_dim(peak_all, tp_index * kv_local, kv_local, 2),
        peak_all,
    )
    local_weighted, local_totals = local_sums(suffix_scores, row_peak, value_rows)
    weighted, totals = prefix_sums(scores, peak_all, prefix_value_rows, chosen)
    parts_weighted = lax.all_to_all(weighted[None], "tp", split_axis=3, concat_axis=0, tiled=True)
    parts_totals = lax.all_to_all(totals[None], "tp", split_axis=3, concat_axis=0, tiled=True)
    prefix_weighted = jnp.sum(parts_weighted, axis=0)
    prefix_totals = jnp.sum(parts_totals, axis=0)
    result = (prefix_weighted + local_weighted) / (prefix_totals + local_totals)[..., None]
    return result.astype(jnp.bfloat16).reshape(row_count, queries.shape[1], queries.shape[2])


def solution(mesh):
    placed = (
        P("rep", None, "tp"),
        P("rep", None, "tp"),
        P("rep", None, "tp"),
        P("rep", None, "tp"),
        P("rep", None, "tp"),
        P("rep"),
        P("rep"),
        P("rep", None),
        P("rep"),
        P("rep"),
        P("rep", None, "tp", None),
        P("rep", None, "tp", None),
    )
    return jax.shard_map(
        shards, mesh=mesh, in_specs=placed, out_specs=P("rep", None, "tp"), check_vma=False
    )
```
